32 devices in a mesh: vtx: 8 (over y, x, core), edg: 4 (over z).
Axes of the slice: x: 2, y: 2, z: 4, core: 2. Of those that a mesh axis runs over, the one named last changes fastest.
Arguments:
- sketch_cols: bfloat16 [131072, 128], P(('vtx', 'edg')), may hold values from -6 to 6
- edge_weight: float32 [131072], P(('vtx', 'edg')), may hold values from 0.25 to 4
- ground: float32 [16384], P('vtx'), may hold values from 0.05 to 0.5
- src_local: int32 [131072], P(('vtx', 'edg')), may hold values from 0 to 2047
- dst_index: int32 [131072], P(('vtx', 'edg')), may hold values from 0 to 2431
- send_rows: int32 [32, 8, 48], P(('vtx', 'edg')), may hold values from 0 to 2047
- edge_count: int32 [32], P(('vtx', 'edg')), may hold values from 512 to 4096, as said below
Outputs:
- solution: float32 [16384, 128], P('vtx')
- resistance: float32 [131072], P(('vtx', 'edg'))
The draws below stay inside these ranges and needn't reach their ends.
Inputs may be any that keep to these rules, and one draw needn't show every extreme that they name: `edge_count`: edge slots of a device at positions of its count or beyond are unused. In every draw some device has all 4096 slots live.
All inputs are finite; a program needn't handle non-finite values.
Results may differ from the reference program's by a relative error of at most 0.0003.
Values sent between devices are 32-bit elements; how exact they have to be, the bound alone decides.
A program may use at most 64 MiB of HBM per device.

```python
import math
import jax
import jax.numpy as jnp
from jax import lax

COLS = 128
VB = 2048
ED = 4096
H = 48
ITERS = 3
GROUPS = 32
V = 16384
EDGES = 131072
N_VTX = 8
N_EDG = 4


def draw_edge_count(key, part):
    mixed = jax.random.fold_in(key, 11)
    first_key, second_key = jax.random.split(mixed)
    powers = jax.random.randint(first_key, (GROUPS,), 0, 4)
    counts = jnp.right_shift(jnp.full((GROUPS,), ED, jnp.int32), powers.astype(jnp.int32))
    chosen = jax.random.randint(second_key, (), 0, GROUPS)
    counts = counts.at[chosen].set(ED)
    return counts.astype(jnp.int32)


def set_ends(array, rng, smallest, high):
    dims = array.shape
    index_at = [jax.random.randint(jax.random.fold_in(rng, axis), (), 0, dims[axis]) for axis in range(len(dims))]
    array = array.at[tuple(index_at)].set(smallest)
    longest = dims.index(max(dims))
    index_at[longest] = (index_at[longest] + 1) % dims[longest]
    return array.at[tuple(index_at)].set(high)


def level_of(own_key, shape, pieces, low, top_value):
    gain = 1.0
    for axis_at, parts in pieces:
        steps = jax.random.uniform(jax.random.fold_in(jax.random.fold_in(own_key, 6), axis_at), (parts,), jnp.float32, low / len(pieces), top_value / len(pieces))
        gain = gain * jnp.repeat(jnp.exp(steps), shape[axis_at] // parts).reshape((-1,) + (1,) * (len(shape) - 1 - axis_at))
    return gain


def gaussian(own_key, extent, deviation, reach, cuts=(), kind=jnp.bfloat16):
    entries = jax.random.normal(own_key, extent, jnp.float32) * deviation
    if len(cuts) > 0:
        entries = level_of(own_key, extent, cuts, -0.22, 0.18) * entries
    return jnp.clip(entries, min=-reach, max=reach).astype(kind)


def setup_inputs(seed: int = 0) -> dict:
    streams_of = jax.random.split(jax.random.key(seed), 8)
    sketch_cols = gaussian(streams_of[0], (EDGES, COLS), 1.0, 6.0, ((0, 32),))
    edge_weight = jnp.clip(jnp.exp(math.log(4.0) - 2.7725887 * jax.random.uniform(streams_of[1], (EDGES,), jnp.float32) ** level_of(streams_of[1], (EDGES,), ((0, 32),), -0.2, 0.2)), 0.25, 4.0)
    ground = jnp.clip(jnp.exp(math.log(0.5) - 2.3025851 * jax.random.uniform(streams_of[2], (V,), jnp.float32) ** level_of(streams_of[2], (V,), ((0, 8),), -0.2, 0.2)), 0.05, 0.5)
    src_local = set_ends(jax.random.randint(streams_of[3], (EDGES,), 0, VB), jax.random.fold_in(streams_of[3], 1), 0, VB - 1).astype(jnp.int32)
    dst_index = set_ends(jax.random.randint(streams_of[4], (EDGES,), 0, VB + N_VTX * H), jax.random.fold_in(streams_of[4], 1), 0, (VB + N_VTX * H) - 1).astype(jnp.int32)
    send_rows = set_ends(jax.random.randint(streams_of[5], (GROUPS, N_VTX, H), 0, VB), jax.random.fold_in(streams_of[5], 1), 0, VB - 1).astype(jnp.int32)
    edge_count = draw_edge_count(jax.random.fold_in(streams_of[7], 71), 0)
    return {"sketch_cols": sketch_cols, "edge_weight": edge_weight, "ground": ground, "src_local": src_local, "dst_index": dst_index, "send_rows": send_rows, "edge_count": edge_count}


lam_low = 0.05
lam_high = 2.0

def chebyshev_terms(steps):
    centre = (lam_high + lam_low) / 2.0
    half_width = (lam_high - lam_low) / 2.0
    sigma_val = centre / half_width
    rho_prev = 1.0 / sigma_val
    pairs = []
    for count_idx in range(steps - 1):
        rho_next = 1.0 / (2.0 * sigma_val - rho_prev)
        pairs.append((rho_next * rho_prev, 2.0 * rho_next / half_width))
        rho_prev = rho_next
    return (1.0 / centre, pairs)

def reference(sketch_cols, edge_weight, ground, src_local, dst_index, send_rows, edge_count):
    vertices = VB * N_VTX
    position = jnp.arange(EDGES, dtype=jnp.int32)
    device = position // ED
    block_id = device // N_EDG
    lane_idx = device % N_EDG
    live_mask = (position % ED < edge_count[device]).astype(jnp.float32)
    source = block_id * VB + src_local
    slot_idx = jnp.maximum(dst_index - VB, 0)
    owner_blk = slot_idx // H
    within = slot_idx % H
    remote = send_rows[owner_blk * N_EDG + lane_idx, block_id, within]
    target = jnp.where(dst_index < VB, block_id * VB + dst_index, owner_blk * VB + remote).astype(jnp.int32)
    weight_live = edge_weight * live_mask
    root_live = jnp.sqrt(edge_weight) * live_mask
    edge_terms = root_live[:, None] * sketch_cols.astype(jnp.float32)
    right_side = jax.ops.segment_sum(edge_terms, source, vertices) - jax.ops.segment_sum(edge_terms, target, vertices)
    degree = jax.ops.segment_sum(weight_live, source, vertices) + jax.ops.segment_sum(weight_live, target, vertices)
    inverse = (1.0 / (degree + ground))[:, None]

    def operate(field_in):
        edge_diffs = weight_live[:, None] * (field_in[source] - field_in[target])
        return ground[:, None] * field_in + jax.ops.segment_sum(edge_diffs, source, vertices) - jax.ops.segment_sum(edge_diffs, target, vertices)
    first, pairs = chebyshev_terms(ITERS)
    residual_now = right_side
    direction = first * inverse * right_side
    solution = jnp.zeros_like(right_side)
    for step_idx in range(ITERS):
        solution = solution + direction
        if step_idx + 1 < ITERS:
            residual_now = residual_now - operate(direction)
            keep_coef, push_coef = pairs[step_idx]
            direction = keep_coef * direction + push_coef * inverse * residual_now
    gaps = solution[source] - solution[target]
    resistance = live_mask * lax.optimization_barrier(jnp.sum(gaps * gaps, axis=1)) / COLS
    return (solution, resistance)
```

```python
import functools

import jax
import jax.numpy as jnp
from jax import lax
from jax.experimental import pallas as pl
from jax.experimental.pallas import tpu as pltpu
from jax.sharding import PartitionSpec as P

ITERS = 3

lam_low = 0.05
lam_high = 2.0
LANES = 128
VMEM_LIMIT = 60 * 1024 * 1024


def chebyshev_terms(steps):
    centre = (lam_high + lam_low) / 2.0
    half_width = (lam_high - lam_low) / 2.0
    sigma_val = centre / half_width
    rho_prev = 1.0 / sigma_val
    pairs = []
    for count_idx in range(steps - 1):
        rho_next = 1.0 / (2.0 * sigma_val - rho_prev)
        pairs.append((rho_next * rho_prev, 2.0 * rho_next / half_width))
        rho_prev = rho_next
    return (1.0 / centre, pairs)


def split2(x):
    hi = x.astype(jnp.bfloat16)
    lo = (x - hi.astype(jnp.float32)).astype(jnp.bfloat16)
    return hi, lo


def split3(x):
    hi = x.astype(jnp.bfloat16)
    rest = x - hi.astype(jnp.float32)
    mid, lo = split2(rest)
    return hi, mid, lo


def signed(src, dst, shape, axis):
    at = lax.broadcasted_iota(jnp.int32, shape, axis)
    value = jnp.where(at == src, 1.0, jnp.where(at == dst, -1.0, 0.0))
    return value.astype(jnp.bfloat16)


def halves(x):
    n = x.shape[1] // 2
    return x[:, :n] + x[:, n:]


def dot(a, b):
    return jnp.dot(a, b, preferred_element_type=jnp.float32)


def load_field(f_ref, h_ref, field):
    rows = f_ref.shape[0]
    field[:rows, :] = jnp.concatenate(split2(f_ref[...]), axis=1)
    field[rows:, :] = jnp.concatenate(split2(h_ref[...]), axis=1)


def scatter(idxr_ref, values, acc):
    tile = values.shape[0]
    hi_lo = jnp.concatenate(split2(values), axis=1)
    dt = signed(idxr_ref[0:1, :], idxr_ref[1:2, :], (acc.shape[0], tile), 0)
    acc[...] += dot(dt, hi_lo)


def start_kernel(sk_ref, colf_ref, coli_ref, idxr_ref, w_ref, y_ref, deg_ref, acc, dacc):
    step = pl.program_id(0)

    @pl.when(step == 0)
    def _():
        acc[...] = jnp.zeros_like(acc)
        dacc[...] = jnp.zeros_like(dacc)

    terms = colf_ref[:, 0:1] * sk_ref[...].astype(jnp.float32)
    scatter(idxr_ref, terms, acc)
    tile = terms.shape[0]
    high = deg_ref.shape[0]
    weights = w_ref[0:1, :]
    up = lax.broadcasted_iota(jnp.int32, (high, tile), 0)
    lane = lax.broadcasted_iota(jnp.int32, (tile, LANES), 1)
    for k in (0, 1):
        row = idxr_ref[2 + k : 3 + k, :]
        picked = jnp.where(up == row // LANES, weights, 0.0)
        low = jnp.where(lane == coli_ref[:, 2 + k : 3 + k] % LANES, 1.0, 0.0).astype(jnp.bfloat16)
        dacc[...] += dot(jnp.concatenate(split3(picked), axis=0), low)

    @pl.when(step == pl.num_programs(0) - 1)
    def _():
        y_ref[...] = halves(acc[...])
        deg_ref[...] = dacc[:high, :] + dacc[high : 2 * high, :] + dacc[2 * high :, :]


def apply_kernel(f_ref, h_ref, colf_ref, coli_ref, idxr_ref, y_ref, field, acc):
    step = pl.program_id(0)

    @pl.when(step == 0)
    def _():
        acc[...] = jnp.zeros_like(acc)
        load_field(f_ref, h_ref, field)

    tile = coli_ref.shape[0]
    d = signed(coli_ref[:, 0:1], coli_ref[:, 1:2], (tile, field.shape[0]), 1)
    flow = halves(dot(d, field[...])) * colf_ref[:, 1:2]
    scatter(idxr_ref, flow, acc)

    @pl.when(step == pl.num_programs(0) - 1)
    def _():
        y_ref[...] = halves(acc[...])


def gap_kernel(f_ref, h_ref, coli_ref, r_ref, field):
    @pl.when(pl.program_id(0) == 0)
    def _():
        load_field(f_ref, h_ref, field)

    tile = coli_ref.shape[0]
    d = signed(coli_ref[:, 0:1], coli_ref[:, 1:2], (tile, field.shape[0]), 1)
    gap = halves(dot(d, field[...]))
    r_ref[...] = jnp.sum(gap * gap, axis=1, keepdims=True)


def whole(x):
    return pl.BlockSpec(x.shape, lambda i: (0,) * x.ndim)


def tiles(x, tile, axis):
    if axis == 0:
        return pl.BlockSpec((tile, x.shape[1]), lambda i: (i, 0))
    return pl.BlockSpec((x.shape[0], tile), lambda i: (0, i))


def params():
    return pltpu.CompilerParams(dimension_semantics=("arbitrary",), vmem_limit_bytes=VMEM_LIMIT)


def local(sketch_cols, edge_weight, ground, src_local, dst_index, send_rows, edge_count):
    blocks = lax.axis_size("vtx")
    num_rows = ground.shape[0]
    num_edges = edge_weight.shape[0]
    slot_width = send_rows.shape[2]
    columns = sketch_cols.shape[1]
    halo_len = blocks * slot_width
    ext = num_rows + halo_len
    tile = min(512, num_edges)
    grid = (num_edges // tile,)
    row_lists = send_rows[0]
    flat_list = row_lists.reshape(-1)
    live_mask = (jnp.arange(num_edges, dtype=jnp.int32) < edge_count[0]).astype(jnp.float32)
    weight_live = edge_weight * live_mask
    root_live = jnp.sqrt(edge_weight) * live_mask
    loop = src_local == dst_index
    src_d = jnp.where(loop, -1, src_local)
    dst_d = jnp.where(loop, -1, dst_index)
    idx = jnp.stack([src_d, dst_d, src_local, dst_index])
    coli = idx.T
    colf = jnp.stack([root_live, weight_live], axis=1)
    w_row = weight_live[None, :]
    high = -(-(ext // LANES) // 16) * 16

    summed, deg = pl.pallas_call(
        start_kernel,
        grid=grid,
        in_specs=[tiles(sketch_cols, tile, 0), tiles(colf, tile, 0), tiles(coli, tile, 0), tiles(idx, tile, 1), tiles(w_row, tile, 1)],
        out_specs=[pl.BlockSpec((ext, columns), lambda i: (0, 0)), pl.BlockSpec((high, LANES), lambda i: (0, 0))],
        out_shape=[jax.ShapeDtypeStruct((ext, columns), jnp.float32), jax.ShapeDtypeStruct((high, LANES), jnp.float32)],
        scratch_shapes=[pltpu.VMEM((ext, 2 * columns), jnp.float32), pltpu.VMEM((3 * high, LANES), jnp.float32)],
        compiler_params=params(),
        name="start",
    )(sketch_cols, colf, coli, idx, w_row)
    degrees = deg.reshape(-1)[:ext]

    def apply_op(field, arrived):
        return pl.pallas_call(
            apply_kernel,
            grid=grid,
            in_specs=[whole(field), whole(arrived), tiles(colf, tile, 0), tiles(coli, tile, 0), tiles(idx, tile, 1)],
            out_specs=pl.BlockSpec((ext, columns), lambda i: (0, 0)),
            out_shape=jax.ShapeDtypeStruct((ext, columns), jnp.float32),
            scratch_shapes=[pltpu.VMEM((ext, 2 * columns), jnp.bfloat16), pltpu.VMEM((ext, 2 * columns), jnp.float32)],
            compiler_params=params(),
            name="apply",
        )(field, arrived, colf, coli, idx)

    def exchange(x):
        return lax.all_to_all(x, "vtx", split_axis=0, concat_axis=0, tiled=True)

    def give_back(total):
        back = exchange(total[num_rows:].reshape(blocks, slot_width, columns))
        return total[:num_rows].at[flat_list].add(back.reshape(halo_len, columns))

    def fetch(field):
        return exchange(field[row_lists]).reshape(halo_len, columns)

    back_degree = exchange(degrees[num_rows:].reshape(blocks, slot_width))
    local_degree = degrees[:num_rows].at[flat_list].add(back_degree.reshape(halo_len))
    first, pairs = chebyshev_terms(ITERS)
    right_side, degree = lax.psum((give_back(summed), local_degree), "edg")
    inverse = (1.0 / (degree + ground))[:, None]
    residual_now = right_side
    direction = first * inverse * right_side
    solution = jnp.zeros_like(right_side)
    for step_idx in range(ITERS):
        solution = solution + direction
        if step_idx + 1 < ITERS:
            flows = lax.psum(give_back(apply_op(direction, fetch(direction))), "edg")
            residual_now = residual_now - (ground[:, None] * direction + flows)
            keep_coef, push_coef = pairs[step_idx]
            direction = keep_coef * direction + push_coef * inverse * residual_now
    arrived = fetch(solution)
    gaps = pl.pallas_call(
        gap_kernel,
        grid=grid,
        in_specs=[whole(solution), whole(arrived), tiles(coli, tile, 0)],
        out_specs=pl.BlockSpec((tile, 1), lambda i: (i, 0)),
        out_shape=jax.ShapeDtypeStruct((num_edges, 1), jnp.float32),
        scratch_shapes=[pltpu.VMEM((ext, 2 * columns), jnp.bfloat16)],
        compiler_params=params(),
        name="gaps",
    )(solution, arrived, coli)
    resistance = live_mask * gaps[:, 0] / columns
    return (solution, resistance)


def solution(mesh):
    in_specs = (
        P(("vtx", "edg"), None),
        P(("vtx", "edg")),
        P("vtx"),
        P(("vtx", "edg")),
        P(("vtx", "edg")),
        P(("vtx", "edg"), None, None),
        P(("vtx", "edg")),
    )
    out_specs = (P("vtx", None), P(("vtx", "edg")))
    return jax.shard_map(local, mesh=mesh, in_specs=in_specs, out_specs=out_specs, check_vma=False)
```

```python
import functools

import jax
import jax.numpy as jnp
from jax import lax
from jax.experimental import pallas as pl
from jax.experimental.pallas import tpu as pltpu
from jax.sharding import PartitionSpec as P

ITERS = 3

lam_low = 0.05
lam_high = 2.0
LANES = 128
VMEM_LIMIT = 60 * 1024 * 1024


def chebyshev_terms(steps):
    centre = (lam_high + lam_low) / 2.0
    half_width = (lam_high - lam_low) / 2.0
    sigma_val = centre / half_width
    rho_prev = 1.0 / sigma_val
    pairs = []
    for count_idx in range(steps - 1):
        rho_next = 1.0 / (2.0 * sigma_val - rho_prev)
        pairs.append((rho_next * rho_prev, 2.0 * rho_next / half_width))
        rho_prev = rho_next
    return (1.0 / centre, pairs)


def split2(x):
    hi = x.astype(jnp.bfloat16)
    lo = (x - hi.astype(jnp.float32)).astype(jnp.bfloat16)
    return hi, lo


def split3(x):
    hi = x.astype(jnp.bfloat16)
    rest = x - hi.astype(jnp.float32)
    mid, lo = split2(rest)
    return hi, mid, lo


def signed(src, dst, shape, axis):
    at = lax.broadcasted_iota(jnp.int32, shape, axis)
    value = jnp.where(at == src, 1.0, jnp.where(at == dst, -1.0, 0.0))
    return value.astype(jnp.bfloat16)


def halves(x):
    n = x.shape[1] // 2
    return x[:, :n] + x[:, n:]


def dot(a, b):
    return jnp.dot(a, b, preferred_element_type=jnp.float32)


def load_field(f_ref, h_ref, field):
    rows = f_ref.shape[0]
    field[:rows, :] = jnp.concatenate(split2(f_ref[...]), axis=1)
    field[rows:, :] = jnp.concatenate(split2(h_ref[...]), axis=1)


def scatter(idxr_ref, values, acc):
    tile = values.shape[0]
    hi_lo = jnp.concatenate(split2(values), axis=1)
    dt = signed(idxr_ref[0:1, :], idxr_ref[1:2, :], (acc.shape[0], tile), 0)
    acc[...] += dot(dt, hi_lo)


def start_kernel(sk_ref, colf_ref, coli_ref, idxr_ref, w_ref, y_ref, deg_ref, acc, dacc):
    step = pl.program_id(0)

    @pl.when(step == 0)
    def _():
        acc[...] = jnp.zeros_like(acc)
        dacc[...] = jnp.zeros_like(dacc)

    terms = colf_ref[:, 0:1] * sk_ref[...].astype(jnp.float32)
    scatter(idxr_ref, terms, acc)
    tile = terms.shape[0]
    high = deg_ref.shape[0]
    weights = w_ref[0:1, :]
    up = lax.broadcasted_iota(jnp.int32, (high, tile), 0)
    lane = lax.broadcasted_iota(jnp.int32, (tile, LANES), 1)
    for k in (0, 1):
        row = idxr_ref[2 + k : 3 + k, :]
        picked = jnp.where(up == row // LANES, weights, 0.0)
        low = jnp.where(lane == coli_ref[:, 2 + k : 3 + k] % LANES, 1.0, 0.0).astype(jnp.bfloat16)
        dacc[...] += dot(jnp.concatenate(split3(picked), axis=0), low)

    @pl.when(step == pl.num_programs(0) - 1)
    def _():
        y_ref[...] = halves(acc[...])
        deg_ref[...] = dacc[:high, :] + dacc[high : 2 * high, :] + dacc[2 * high :, :]


def apply_kernel(f_ref, h_ref, colf_ref, coli_ref, idxr_ref, y_ref, field, acc):
    step = pl.program_id(0)

    @pl.when(step == 0)
    def _():
        acc[...] = jnp.zeros_like(acc)
        load_field(f_ref, h_ref, field)

    tile = coli_ref.shape[0]
    d = signed(coli_ref[:, 0:1], coli_ref[:, 1:2], (tile, field.shape[0]), 1)
    flow = halves(dot(d, field[...])) * colf_ref[:, 1:2]
    scatter(idxr_ref, flow, acc)

    @pl.when(step == pl.num_programs(0) - 1)
    def _():
        y_ref[...] = halves(acc[...])


def gap_kernel(f_ref, h_ref, coli_ref, r_ref, field):
    @pl.when(pl.program_id(0) == 0)
    def _():
        load_field(f_ref, h_ref, field)

    tile = coli_ref.shape[0]
    d = signed(coli_ref[:, 0:1], coli_ref[:, 1:2], (tile, field.shape[0]), 1)
    gap = halves(dot(d, field[...]))
    r_ref[...] = jnp.sum(gap * gap, axis=1, keepdims=True)


def slot_copy(src, dst, send_sem, recv_sem, target):
    return pltpu.make_async_remote_copy(
        src_ref=src, dst_ref=dst, send_sem=send_sem, recv_sem=recv_sem,
        device_id=target, device_id_type=pl.DeviceIdType.MESH,
    )


def all_to_all(me, peers, src, dst, send_sem, recv_sem):
    for off in range(1, peers):
        to = lax.rem(me + off, peers)
        slot_copy(src(to), dst.at[me], send_sem.at[off], recv_sem.at[off], {"vtx": to}).start()


def all_to_all_wait(me, peers, src, dst, send_sem, recv_sem):
    for off in range(1, peers):
        to = lax.rem(me + off, peers)
        origin = lax.rem(me + peers - off, peers)
        slot_copy(src(to), dst.at[origin], send_sem.at[off], recv_sem.at[off], {"vtx": to}).wait()


def line_sum(z, pieces, own, outer, inner, mine, result, send_sem, outer_sem, inner_sem):
    count = len(pieces)

    def copy(kind, k, src, dst, sem, target):
        rows = pl.ds(*pieces[k])
        return slot_copy(src.at[rows], dst.at[rows], send_sem.at[kind, k], sem.at[k], {"edg": target})

    @pl.when((z + 1) // 2 % 2 == 0)
    def _():
        near = 1 + z // 3
        for k in range(count):
            copy(0, k, own, outer, outer_sem, near).start()
        for k in range(count):
            copy(0, k, own, outer, outer_sem, near).wait_recv()
            rows = pl.ds(*pieces[k])
            result[rows, :] = outer[rows, :]
        for k in range(count):
            copy(0, k, own, outer, outer_sem, near).wait_send()

    def middle(side):
        far, peer = 3 * side, 2 - side
        lag_total, lag_pass = 2, 4
        for t in range(count + lag_pass):
            if t < count:
                rows = pl.ds(*pieces[t])
                copy(1, t, own, outer, outer_sem, far).wait_recv()
                if t % 2 != side:
                    mine[rows, :] = own[rows, :] + outer[rows, :]
                    copy(0, t, mine, inner, inner_sem, peer).start()
            k = t - lag_total
            if 0 <= k < count and k % 2 == side:
                rows = pl.ds(*pieces[k])
                copy(0, k, mine, inner, inner_sem, peer).wait_recv()
                total = (own[rows, :] + outer[rows, :]) + inner[rows, :]
                mine[rows, :] = total
                copy(0, k, mine, inner, inner_sem, peer).start()
                copy(1, k, mine, outer, outer_sem, far).start()
                result[rows, :] = total
            k = t - lag_pass
            if 0 <= k < count and k % 2 != side:
                rows = pl.ds(*pieces[k])
                copy(0, k, mine, inner, inner_sem, peer).wait_recv()
                copy(1, k, inner, outer, outer_sem, far).start()
                result[rows, :] = inner[rows, :]
        for k in range(count):
            copy(0, k, mine, inner, inner_sem, peer).wait_send()
            copy(1, k, mine if k % 2 == side else inner, outer, outer_sem, far).wait_send()

    for side in (0, 1):
        pl.when(z == 1 + side)(functools.partial(middle, side))


def stage_kernel(stage, peers, pieces, *refs):
    first, pairs = chebyshev_terms(ITERS)
    last = stage == ITERS - 1
    refs = list(refs)

    def take(n):
        got = refs[:n]
        del refs[:n]
        return got

    y_ref, rows_smem, list_ref, ground_ref = take(4)
    if stage == 0:
        deg_ref, degh_ref, padrow_ref, padcol_ref = take(4)
    else:
        res_in, dir_in, inv_in = take(3)
        sol_in = take(1)[0] if stage > 1 else dir_in
    if stage == 0:
        dir_ref, res_ref, inv_ref, arr_ref = take(4)
        listed_from = dir_ref
    elif not last:
        dir_ref, res_ref, sol_ref, arr_ref = take(4)
        listed_from = dir_ref
    else:
        sol_ref, arr_ref = take(2)
        listed_from = sol_ref
    own, outer, inner, mine, result, back, listed, landed = take(8)
    back_send, back_recv, land_send, land_recv, line_send, outer_sem, inner_sem = take(7)
    if stage == 0:
        dback, dback_send, dback_recv = take(3)

    me, z = lax.axis_index("vtx"), lax.axis_index("edg")
    slot = back.shape[1]
    num_rows = ground_ref.shape[0]
    columns = y_ref.shape[1]
    middle = (z + 1) // 2 % 2

    barrier = pltpu.get_barrier_semaphore()

    def greet(target):
        pl.semaphore_signal(barrier, inc=1, device_id=target, device_id_type=pl.DeviceIdType.MESH)

    for off in range(1, peers):
        greet({"vtx": lax.rem(me + off, peers)})

    @pl.when(z > 0)
    def _():
        greet({"edg": z - 1})

    @pl.when(z < 3)
    def _():
        greet({"edg": z + 1})

    pl.semaphore_wait(barrier, peers + middle)

    def halo_of(to):
        return y_ref.at[pl.ds(pl.multiple_of(num_rows + to * slot, 8), slot)]

    def degree_of(to):
        return degh_ref.at[to]

    all_to_all(me, peers, halo_of, back, back_send, back_recv)
    if stage == 0:
        all_to_all(me, peers, degree_of, dback, dback_send, dback_recv)
    back[me] = y_ref[pl.ds(pl.multiple_of(num_rows + me * slot, 8), slot), :]
    if stage == 0:
        dback[me] = degh_ref[me]
    all_to_all_wait(me, peers, halo_of, back, back_send, back_recv)
    returned = jnp.concatenate(split2(back[...].reshape(peers * slot, columns)), axis=1)
    step = 256 if num_rows % 256 == 0 else num_rows
    for at in range(0, num_rows, step):
        row = lax.broadcasted_iota(jnp.int32, (step, peers * slot), 0) + at
        pick = jnp.where(row == list_ref[...], 1.0, 0.0).astype(jnp.bfloat16)
        own[at : at + step, :] = y_ref[at : at + step, :] + halves(dot(pick, returned))
    if stage == 0:
        all_to_all_wait(me, peers, degree_of, dback, dback_send, dback_recv)
        high = num_rows // LANES
        values = jnp.concatenate([dback[q, 0:1, :] for q in range(peers)], axis=1)
        up = lax.broadcasted_iota(jnp.int32, (high, values.shape[1]), 0)
        picked = jnp.where(up == padrow_ref[...] // LANES, values, 0.0)
        lane = lax.broadcasted_iota(jnp.int32, (values.shape[1], LANES), 1)
        low = jnp.where(lane == padcol_ref[...] % LANES, 1.0, 0.0).astype(jnp.bfloat16)
        parts = dot(jnp.concatenate(split3(picked), axis=0), low)
        own[num_rows:, :] = deg_ref[:high, :] + (parts[:high] + parts[high : 2 * high] + parts[2 * high :])

    line_sum(z, pieces, own, outer, inner, mine, result, line_send, outer_sem, inner_sem)

    eye = lax.broadcasted_iota(jnp.int32, (LANES, LANES), 0) == lax.broadcasted_iota(jnp.int32, (LANES, LANES), 1)
    for at in range(0, num_rows, LANES):
        rows = slice(at, at + LANES)
        if stage == 0:
            row = at // LANES
            degree = result[num_rows + row : num_rows + row + 1, :]
            column = jnp.sum(jnp.where(eye, degree, 0.0), axis=1, keepdims=True)
            inverse = 1.0 / (column + ground_ref[rows, :])
            inv_ref[rows, :] = inverse
            res_ref[rows, :] = result[rows, :]
            dir_ref[rows, :] = first * inverse * result[rows, :]
        else:
            keep_coef, push_coef = pairs[stage - 1]
            residual = res_in[rows, :] - (ground_ref[rows, :] * dir_in[rows, :] + result[rows, :])
            direction = keep_coef * dir_in[rows, :] + push_coef * inv_in[rows, :] * residual
            if not last:
                res_ref[rows, :] = residual
                dir_ref[rows, :] = direction
            sol_ref[rows, :] = sol_in[rows, :] + direction

    def pick_rows(h, _):
        for q in range(peers):
            listed[q, pl.ds(h, 1), :] = listed_from[pl.ds(rows_smem[q, h], 1), :]
        return 0

    lax.fori_loop(0, slot, pick_rows, 0)

    def listed_of(to):
        return listed.at[to]

    all_to_all(me, peers, listed_of, landed, land_send, land_recv)
    landed[me] = listed[me]
    all_to_all_wait(me, peers, listed_of, landed, land_send, land_recv)
    arr_ref[...] = landed[...].reshape(peers * slot, columns)


def run_stage(stage, peers, slot, num_rows, columns, operands):
    extra = num_rows // LANES if stage == 0 else 0
    size = 128
    pieces = [(num_rows, extra)] if extra else []
    pieces += [(at, size) for at in range(0, num_rows, size)]
    count = len(pieces)
    total = num_rows + extra
    f32 = jnp.float32
    field = jax.ShapeDtypeStruct((num_rows, columns), f32)
    arrived = jax.ShapeDtypeStruct((peers * slot, columns), f32)
    if stage == 0:
        outs = [field, field, jax.ShapeDtypeStruct((num_rows, 1), f32), arrived]
    elif stage < ITERS - 1:
        outs = [field, field, field, arrived]
    else:
        outs = [field, arrived]
    vmem = pl.BlockSpec(memory_space=pltpu.VMEM)
    in_specs = [vmem] * len(operands)
    in_specs[1] = pl.BlockSpec(memory_space=pltpu.SMEM)
    dma = pltpu.SemaphoreType.DMA
    buffer = pltpu.VMEM((total, columns), f32)
    halo = pltpu.VMEM((peers, slot, columns), f32)
    scratch = [buffer] * 5 + [halo] * 3
    scratch += [dma((peers,))] * 4 + [dma((2, count)), dma((count,)), dma((count,))]
    if stage == 0:
        scratch += [pltpu.VMEM((peers, 8, LANES), f32), dma((peers,)), dma((peers,))]
    return pl.pallas_call(
        functools.partial(stage_kernel, stage, peers, pieces),
        in_specs=in_specs,
        out_specs=[vmem] * len(outs),
        out_shape=outs,
        scratch_shapes=scratch,
        compiler_params=pltpu.CompilerParams(collective_id=stage, has_side_effects=True, vmem_limit_bytes=VMEM_LIMIT),
        name="stage%d" % stage,
    )(*operands)


def whole(x):
    return pl.BlockSpec(x.shape, lambda i: (0,) * x.ndim)


def tiles(x, tile, axis):
    if axis == 0:
        return pl.BlockSpec((tile, x.shape[1]), lambda i: (i, 0))
    return pl.BlockSpec((x.shape[0], tile), lambda i: (0, i))


def params():
    return pltpu.CompilerParams(dimension_semantics=("arbitrary",), vmem_limit_bytes=VMEM_LIMIT)


def local(sketch_cols, edge_weight, ground, src_local, dst_index, send_rows, edge_count):
    blocks = lax.axis_size("vtx")
    num_rows = ground.shape[0]
    num_edges = edge_weight.shape[0]
    slot_width = send_rows.shape[2]
    columns = sketch_cols.shape[1]
    halo_len = blocks * slot_width
    ext = num_rows + halo_len
    tile = min(512, num_edges)
    grid = (num_edges // tile,)
    row_lists = send_rows[0]
    flat_list = row_lists.reshape(-1)
    live_mask = (jnp.arange(num_edges, dtype=jnp.int32) < edge_count[0]).astype(jnp.float32)
    weight_live = edge_weight * live_mask
    root_live = jnp.sqrt(edge_weight) * live_mask
    loop = src_local == dst_index
    src_d = jnp.where(loop, -1, src_local)
    dst_d = jnp.where(loop, -1, dst_index)
    idx = jnp.stack([src_d, dst_d, src_local, dst_index])
    coli = idx.T
    colf = jnp.stack([root_live, weight_live], axis=1)
    w_row = weight_live[None, :]
    high = -(-(ext // LANES) // 16) * 16

    summed, deg = pl.pallas_call(
        start_kernel,
        grid=grid,
        in_specs=[tiles(sketch_cols, tile, 0), tiles(colf, tile, 0), tiles(coli, tile, 0), tiles(idx, tile, 1), tiles(w_row, tile, 1)],
        out_specs=[pl.BlockSpec((ext, columns), lambda i: (0, 0)), pl.BlockSpec((high, LANES), lambda i: (0, 0))],
        out_shape=[jax.ShapeDtypeStruct((ext, columns), jnp.float32), jax.ShapeDtypeStruct((high, LANES), jnp.float32)],
        scratch_shapes=[pltpu.VMEM((ext, 2 * columns), jnp.float32), pltpu.VMEM((3 * high, LANES), jnp.float32)],
        compiler_params=params(),
        name="start",
    )(sketch_cols, colf, coli, idx, w_row)

    def apply_op(field, arrived):
        return pl.pallas_call(
            apply_kernel,
            grid=grid,
            in_specs=[whole(field), whole(arrived), tiles(colf, tile, 0), tiles(coli, tile, 0), tiles(idx, tile, 1)],
            out_specs=pl.BlockSpec((ext, columns), lambda i: (0, 0)),
            out_shape=jax.ShapeDtypeStruct((ext, columns), jnp.float32),
            scratch_shapes=[pltpu.VMEM((ext, 2 * columns), jnp.bfloat16), pltpu.VMEM((ext, 2 * columns), jnp.float32)],
            compiler_params=params(),
            name="apply",
        )(field, arrived, colf, coli, idx)

    flat_row = flat_list[None, :]
    ground_col = ground[:, None]
    pad_list = jnp.pad(row_lists, ((0, 0), (0, LANES - slot_width)), constant_values=-1).reshape(-1)
    degrees = jnp.pad(deg.reshape(-1)[num_rows:ext].reshape(blocks, slot_width), ((0, 0), (0, LANES - slot_width)))
    degree_out = jnp.broadcast_to(degrees[:, None, :], (blocks, 8, LANES))
    stage = functools.partial(run_stage, peers=blocks, slot=slot_width, num_rows=num_rows, columns=columns)
    common = (row_lists, flat_row, ground_col)
    direction, residual, inverse, arrived = stage(
        0, operands=(summed,) + common + (deg, degree_out, pad_list[None, :], pad_list[:, None])
    )
    state = (residual, direction, inverse)
    for step_idx in range(1, ITERS):
        summed = apply_op(direction, arrived)
        if step_idx < ITERS - 1:
            direction, residual, solution, arrived = stage(step_idx, operands=(summed,) + common + state)
            state = (residual, direction, inverse, solution)
        else:
            solution, arrived = stage(step_idx, operands=(summed,) + common + state)
    gaps = pl.pallas_call(
        gap_kernel,
        grid=grid,
        in_specs=[whole(solution), whole(arrived), tiles(coli, tile, 0)],
        out_specs=pl.BlockSpec((tile, 1), lambda i: (i, 0)),
        out_shape=jax.ShapeDtypeStruct((num_edges, 1), jnp.float32),
        scratch_shapes=[pltpu.VMEM((ext, 2 * columns), jnp.bfloat16)],
        compiler_params=params(),
        name="gaps",
    )(solution, arrived, coli)
    resistance = live_mask * gaps[:, 0] / columns
    return (solution, resistance)


def solution(mesh):
    in_specs = (
        P(("vtx", "edg"), None),
        P(("vtx", "edg")),
        P("vtx"),
        P(("vtx", "edg")),
        P(("vtx", "edg")),
        P(("vtx", "edg"), None, None),
        P(("vtx", "edg")),
    )
    out_specs = (P("vtx", None), P(("vtx", "edg")))
    return jax.shard_map(local, mesh=mesh, in_specs=in_specs, out_specs=out_specs, check_vma=False)
```

```python
import functools

import jax
import jax.numpy as jnp
from jax import lax
from jax.experimental import pallas as pl
from jax.experimental.pallas import tpu as pltpu
from jax.sharding import PartitionSpec as P

ITERS = 3

lam_low = 0.05
lam_high = 2.0
LANES = 128
VMEM_LIMIT = 60 * 1024 * 1024


def chebyshev_terms(steps):
    centre = (lam_high + lam_low) / 2.0
    half_width = (lam_high - lam_low) / 2.0
    sigma_val = centre / half_width
    rho_prev = 1.0 / sigma_val
    pairs = []
    for count_idx in range(steps - 1):
        rho_next = 1.0 / (2.0 * sigma_val - rho_prev)
        pairs.append((rho_next * rho_prev, 2.0 * rho_next / half_width))
        rho_prev = rho_next
    return (1.0 / centre, pairs)


def split2(x):
    hi = x.astype(jnp.bfloat16)
    lo = (x - hi.astype(jnp.float32)).astype(jnp.bfloat16)
    return hi, lo


def split3(x):
    hi = x.astype(jnp.bfloat16)
    rest = x - hi.astype(jnp.float32)
    mid, lo = split2(rest)
    return hi, mid, lo


def signed(src, dst, shape, axis):
    at = lax.broadcasted_iota(jnp.int32, shape, axis)
    value = jnp.where(at == src, 1.0, jnp.where(at == dst, -1.0, 0.0))
    return value.astype(jnp.bfloat16)


def halves(x):
    n = x.shape[1] // 2
    return x[:, :n] + x[:, n:]


def dot(a, b):
    return jnp.dot(a, b, preferred_element_type=jnp.float32)


def even_piece(total, most):
    return max(n for n in range(8, most + 1, 8) if total % n == 0)


def slot_copy(src, dst, send_sem, recv_sem, target):
    return pltpu.make_async_remote_copy(
        src_ref=src, dst_ref=dst, send_sem=send_sem, recv_sem=recv_sem,
        device_id=target, device_id_type=pl.DeviceIdType.MESH,
    )


def all_to_all(me, peers, src, dst, send_sem, recv_sem):
    for off in range(1, peers):
        to = lax.rem(me + off, peers)
        slot_copy(src(to), dst.at[me], send_sem.at[off], recv_sem.at[off], {"vtx": to}).start()


def all_to_all_wait(me, peers, src, dst, send_sem, recv_sem):
    for off in range(1, peers):
        to = lax.rem(me + off, peers)
        origin = lax.rem(me + peers - off, peers)
        slot_copy(src(to), dst.at[origin], send_sem.at[off], recv_sem.at[off], {"vtx": to}).wait()


class LineSum:
    lag_total, lag_pass = 2, 4

    def __init__(self, z, pieces, own, outer, inner, mine, result, send_sem, outer_sem, inner_sem):
        self.z, self.pieces, self.own, self.outer, self.inner = z, pieces, own, outer, inner
        self.mine, self.result, self.send_sem = mine, result, send_sem
        self.outer_sem, self.inner_sem = outer_sem, inner_sem
        self.near = 1 + z // 3

    def copy(self, kind, k, src, dst, sem, target):
        rows = pl.ds(*self.pieces[k])
        return slot_copy(src.at[rows], dst.at[rows], self.send_sem.at[kind, k], sem.at[k], {"edg": target})

    def end_copy(self, k):
        return self.copy(0, k, self.own, self.outer, self.outer_sem, self.near)

    def at_end(self, work):
        pl.when((self.z + 1) // 2 % 2 == 0)(work)

    def at_middle(self, work):
        for side in (0, 1):
            pl.when(self.z == 1 + side)(functools.partial(work, side))

    def send_group(self, ks):
        def work():
            for k in ks:
                self.end_copy(k).start()

        self.at_end(work)

    def step(self, side, t):
        own, outer, inner, mine, result = self.own, self.outer, self.inner, self.mine, self.result
        count = len(self.pieces)
        far, peer = 3 * side, 2 - side
        if t < count:
            rows = pl.ds(*self.pieces[t])
            self.copy(1, t, own, outer, self.outer_sem, far).wait_recv()
            if t % 2 != side:
                mine[rows, :] = own[rows, :] + outer[rows, :]
                self.copy(0, t, mine, inner, self.inner_sem, peer).start()
        k = t - self.lag_total
        if 0 <= k < count and k % 2 == side:
            rows = pl.ds(*self.pieces[k])
            self.copy(0, k, mine, inner, self.inner_sem, peer).wait_recv()
            total = (own[rows, :] + outer[rows, :]) + inner[rows, :]
            mine[rows, :] = total
            self.copy(0, k, mine, inner, self.inner_sem, peer).start()
            self.copy(1, k, mine, outer, self.outer_sem, far).start()
            result[rows, :] = total
        k = t - self.lag_pass
        if 0 <= k < count and k % 2 != side:
            rows = pl.ds(*self.pieces[k])
            self.copy(0, k, mine, inner, self.inner_sem, peer).wait_recv()
            self.copy(1, k, inner, outer, self.outer_sem, far).start()
            result[rows, :] = inner[rows, :]

    def pass_group(self, ts):
        def work(side):
            for t in ts:
                self.step(side, t)

        self.at_middle(work)

    def finish(self):
        count = len(self.pieces)

        def end():
            for k in range(count):
                self.end_copy(k).wait_recv()
                rows = pl.ds(*self.pieces[k])
                self.result[rows, :] = self.outer[rows, :]
            for k in range(count):
                self.end_copy(k).wait_send()

        def middle(side):
            for k in range(count):
                self.copy(0, k, self.mine, self.inner, self.inner_sem, 2 - side).wait_send()
                source = self.mine if k % 2 == side else self.inner
                self.copy(1, k, source, self.outer, self.outer_sem, 3 * side).wait_send()

        self.at_end(end)
        self.at_middle(middle)


def stage_kernel(stage, peers, groups, pieces, *refs):
    first, pairs = chebyshev_terms(ITERS)
    last = stage == ITERS - 1
    refs = list(refs)

    def take(n):
        got = refs[:n]
        del refs[:n]
        return got

    g_ref, rows_smem, idx_ref, flt_ref, list_ref, ground_ref = take(6)
    if stage == 0:
        (list8_ref,) = take(1)
    else:
        res_in, dir_in, inv_in = take(3)
        sol_in = take(1)[0] if stage > 1 else dir_in
    if stage == 0:
        dir_ref, res_ref, inv_ref, gout_ref = take(4)
        listed_from = dir_ref
    elif not last:
        dir_ref, res_ref, sol_ref, gout_ref = take(4)
        listed_from = dir_ref
    else:
        sol_ref, gap_ref = take(2)
        listed_from = sol_ref
    own, outer, inner, mine, result, yhalo, back, listed, landed = take(9)
    idxc, fltc, field, part, retb, acc = take(6)
    back_send, back_recv, land_send, land_recv, line_send, outer_sem, inner_sem = take(7)
    if stage == 0:
        flows, degh, dback, dback_send, dback_recv = take(5)
    else:
        flows = g_ref

    me, z = lax.axis_index("vtx"), lax.axis_index("edg")
    slot, columns = back.shape[1], back.shape[2]
    halo_len = peers * slot
    num_rows = ground_ref.shape[0] * LANES
    num_edges = idx_ref.shape[1]
    etile = min(512, num_edges)
    ktile = min(1024, num_edges)

    barrier = pltpu.get_barrier_semaphore()

    def greet(target):
        pl.semaphore_signal(barrier, inc=1, device_id=target, device_id_type=pl.DeviceIdType.MESH)

    for off in range(1, peers):
        greet({"vtx": lax.rem(me + off, peers)})

    @pl.when(z > 0)
    def _():
        greet({"edg": z - 1})

    @pl.when(z < 3)
    def _():
        greet({"edg": z + 1})

    idxc[...] = idx_ref[...].T
    fltc[...] = flt_ref[...].T

    if stage == 0:

        def make_terms(k, _):
            rows = pl.ds(pl.multiple_of(k * etile, etile), etile)
            terms = fltc[rows, 0:1] * g_ref[rows, :].astype(jnp.float32)
            flows[rows, :] = jnp.concatenate(split2(terms), axis=1)
            return 0

        lax.fori_loop(0, num_edges // etile, make_terms, 0)
        weights = flt_ref[1:2, :]
        lane = lax.broadcasted_iota(jnp.int32, (num_edges, LANES), 1)

        def count_up(high, row, column):
            up = lax.broadcasted_iota(jnp.int32, (high, num_edges), 0)
            picked = jnp.where(up == row, weights, 0.0)
            low = jnp.where(lane == column, 1.0, 0.0).astype(jnp.bfloat16)
            parts = dot(jnp.concatenate(split3(picked), axis=0), low)
            return parts[:high] + parts[high : 2 * high] + parts[2 * high :]

        high = num_rows // LANES
        up_rows = -(-high // 16) * 16
        degree_own = count_up(up_rows, idx_ref[2:3, :] // LANES, idxc[:, 2:3] % LANES)
        degree_own += count_up(up_rows, idx_ref[3:4, :] // LANES, idxc[:, 3:4] % LANES)
        own[num_rows:, :] = degree_own[:high]
        degree_far = count_up(-(-peers // 16) * 16, idx_ref[4:5, :], idxc[:, 5:6])
        for q in range(peers):
            degh[q] = jnp.broadcast_to(degree_far[q : q + 1, :], (8, LANES))

    def scatter_rows(at, rows):
        acc[:rows, :] = jnp.zeros((rows, 2 * columns), jnp.float32)

        def body(k, _):
            cols = pl.ds(pl.multiple_of(k * ktile, ktile), ktile)
            pick = signed(idx_ref[0:1, cols] - at, idx_ref[1:2, cols] - at, (rows, ktile), 0)
            acc[:rows, :] += dot(pick, flows[cols, :])
            return 0

        lax.fori_loop(0, num_edges // ktile, body, 0)
        return halves(acc[:rows, :])

    hpiece = even_piece(halo_len, 512)
    for at in range(0, halo_len, hpiece):
        yhalo[at : at + hpiece, :] = scatter_rows(num_rows + at, hpiece)

    pl.semaphore_wait(barrier, peers + (z + 1) // 2 % 2)

    def halo_of(to):
        return yhalo.at[pl.ds(pl.multiple_of(to * slot, 8), slot)]

    def degree_of(to):
        return degh.at[to]

    all_to_all(me, peers, halo_of, back, back_send, back_recv)
    back[me] = yhalo[pl.ds(pl.multiple_of(me * slot, 8), slot), :]
    if stage == 0:
        all_to_all(me, peers, degree_of, dback, dback_send, dback_recv)
        dback[me] = degh[me]

    line = LineSum(z, pieces, own, outer, inner, mine, result, line_send, outer_sem, inner_sem)
    for c, (at, size, ks) in enumerate(groups):
        local_sum = scatter_rows(at, size)
        if c == 0:
            all_to_all_wait(me, peers, halo_of, back, back_send, back_recv)
            retb[...] = jnp.concatenate(split2(back[...].reshape(halo_len, columns)), axis=1)
            if stage == 0:
                all_to_all_wait(me, peers, degree_of, dback, dback_send, dback_recv)
                cols8 = list8_ref[...].T
                up = lax.broadcasted_iota(jnp.int32, (high, LANES), 0)
                lane = lax.broadcasted_iota(jnp.int32, (LANES, LANES), 1)
                for q in range(peers):
                    picked = jnp.where(up == list8_ref[q : q + 1, :] // LANES, dback[q, 0:1, :], 0.0)
                    low = jnp.where(lane == cols8[:, q : q + 1] % LANES, 1.0, 0.0).astype(jnp.bfloat16)
                    parts = dot(jnp.concatenate(split3(picked), axis=0), low)
                    own[num_rows:, :] += parts[:high] + parts[high : 2 * high] + parts[2 * high :]
        row = lax.broadcasted_iota(jnp.int32, (size, halo_len), 0)
        pick = jnp.where(row == list_ref[...] - at, 1.0, 0.0).astype(jnp.bfloat16)
        own[at : at + size, :] = local_sum + halves(dot(pick, retb[...]))
        line.send_group(ks)
        if c > 0:
            line.pass_group(groups[c - 1][2])
    line.pass_group(list(groups[-1][2]) + list(range(len(pieces), len(pieces) + line.lag_pass)))
    line.finish()

    ground_cols = ground_ref[...].T
    if stage == 0:
        inverse = 1.0 / (result[num_rows:, :] + ground_ref[...])
        inv_ref[...] = inverse
    else:
        inverse = inv_in[...]
    inverse_cols = inverse.T
    for at in range(0, num_rows, LANES):
        rows = slice(at, at + LANES)
        j = at // LANES
        inv_col, ground_col = inverse_cols[:, j : j + 1], ground_cols[:, j : j + 1]
        if stage == 0:
            res_ref[rows, :] = result[rows, :]
            shown = first * inv_col * result[rows, :]
            dir_ref[rows, :] = shown
        else:
            keep_coef, push_coef = pairs[stage - 1]
            residual = res_in[rows, :] - (ground_col * dir_in[rows, :] + result[rows, :])
            direction = keep_coef * dir_in[rows, :] + push_coef * inv_col * residual
            total = sol_in[rows, :] + direction
            sol_ref[rows, :] = total
            shown = total
            if not last:
                res_ref[rows, :] = residual
                dir_ref[rows, :] = direction
                shown = direction
        field[rows, :] = jnp.concatenate(split2(shown), axis=1)

    def pick_rows(h, _):
        for q in range(peers):
            listed[q, pl.ds(h, 1), :] = listed_from[pl.ds(rows_smem[q, h], 1), :]
        return 0

    lax.fori_loop(0, slot, pick_rows, 0)

    def listed_of(to):
        return listed.at[to]

    all_to_all(me, peers, listed_of, landed, land_send, land_recv)
    landed[me] = listed[me]

    def gather_near(k, _):
        rows = pl.ds(pl.multiple_of(k * etile, etile), etile)
        d = signed(idxc[rows, 0:1], idxc[rows, 1:2], (etile, num_rows), 1)
        part[rows, :] = halves(dot(d, field[:num_rows, :]))
        return 0

    lax.fori_loop(0, num_edges // etile, gather_near, 0)
    all_to_all_wait(me, peers, listed_of, landed, land_send, land_recv)
    field[num_rows:, :] = jnp.concatenate(split2(landed[...].reshape(halo_len, columns)), axis=1)

    def gather_far(k):
        rows = pl.ds(k * etile, etile)
        d = signed(idxc[rows, 0:1] - num_rows, idxc[rows, 1:2] - num_rows, (etile, halo_len), 1)
        return rows, part[rows, :] + halves(dot(d, field[num_rows:, :]))

    if not last:

        def make_flows(k, _):
            k = pl.multiple_of(k * etile, etile) // etile
            rows, gap = gather_far(k)
            gout_ref[rows, :] = jnp.concatenate(split2(gap * fltc[rows, 1:2]), axis=1)
            return 0

        lax.fori_loop(0, num_edges // etile, make_flows, 0)
    else:
        lane = lax.broadcasted_iota(jnp.int32, (LANES, LANES), 1)
        wide = num_edges // LANES
        for base in range(0, wide, LANES):
            sums = jnp.zeros((LANES, LANES), jnp.float32)
            for k in range(base * LANES // etile, min(wide, base + LANES) * LANES // etile):
                _, gap = gather_far(k)
                square = jnp.sum(gap * gap, axis=1, keepdims=True)
                for i in range(etile // LANES):
                    j = k * (etile // LANES) + i - base
                    sums = jnp.where(lane == j, square[i * LANES : (i + 1) * LANES, :], sums)
            take_rows = min(LANES, wide - base)
            gap_ref[base : base + take_rows, :] = sums.T[:take_rows, :]


def run_stage(stage, peers, slot, num_rows, columns, num_edges, operands):
    high = num_rows // LANES
    extra = high if stage == 0 else 0
    size, big = 128, 512
    pieces = [(at, size) for at in range(0, num_rows, size)]
    groups = [[at, big, list(range(at // size, (at + big) // size))] for at in range(0, num_rows, big)]
    if extra:
        groups[-1][2].append(len(pieces))
        pieces.append((num_rows, extra))
    count = len(pieces)
    f32, bf16, i32 = jnp.float32, jnp.bfloat16, jnp.int32
    halo_len = peers * slot
    field = jax.ShapeDtypeStruct((num_rows, columns), f32)
    flows = jax.ShapeDtypeStruct((num_edges, 2 * columns), bf16)
    if stage == 0:
        outs = [field, field, jax.ShapeDtypeStruct((high, LANES), f32), flows]
    elif stage < ITERS - 1:
        outs = [field, field, field, flows]
    else:
        outs = [field, jax.ShapeDtypeStruct((num_edges // LANES, LANES), f32)]
    vmem = pl.BlockSpec(memory_space=pltpu.VMEM)
    in_specs = [vmem] * len(operands)
    in_specs[1] = pl.BlockSpec(memory_space=pltpu.SMEM)
    dma = pltpu.SemaphoreType.DMA
    buffer = pltpu.VMEM((num_rows + extra, columns), f32)
    halo = pltpu.VMEM((peers, slot, columns), f32)
    scratch = [buffer] * 5 + [pltpu.VMEM((halo_len, columns), f32)] + [halo] * 3
    scratch += [pltpu.VMEM((num_edges, 8), i32), pltpu.VMEM((num_edges, 8), f32)]
    scratch += [pltpu.VMEM((num_rows + halo_len, 2 * columns), bf16), pltpu.VMEM((num_edges, columns), f32)]
    scratch += [pltpu.VMEM((halo_len, 2 * columns), bf16), pltpu.VMEM((big, 2 * columns), f32)]
    scratch += [dma((peers,))] * 4 + [dma((2, count)), dma((count,)), dma((count,))]
    if stage == 0:
        scratch += [pltpu.VMEM((num_edges, 2 * columns), bf16)]
        scratch += [pltpu.VMEM((peers, 8, LANES), f32)] * 2 + [dma((peers,)), dma((peers,))]
    return pl.pallas_call(
        functools.partial(stage_kernel, stage, peers, groups, pieces),
        in_specs=in_specs,
        out_specs=[vmem] * len(outs),
        out_shape=outs,
        scratch_shapes=scratch,
        compiler_params=pltpu.CompilerParams(collective_id=stage, has_side_effects=True, vmem_limit_bytes=VMEM_LIMIT),
        name="stage%d" % stage,
    )(*operands)


def local(sketch_cols, edge_weight, ground, src_local, dst_index, send_rows, edge_count):
    blocks = lax.axis_size("vtx")
    num_rows = ground.shape[0]
    num_edges = edge_weight.shape[0]
    slot_width = send_rows.shape[2]
    columns = sketch_cols.shape[1]
    row_lists = send_rows[0]
    live_mask = (jnp.arange(num_edges, dtype=jnp.int32) < edge_count[0]).astype(jnp.float32)
    weight_live = edge_weight * live_mask
    root_live = jnp.sqrt(edge_weight) * live_mask
    loop = src_local == dst_index
    slots = dst_index - num_rows
    peer = jnp.where(slots < 0, -1, slots // slot_width)
    within = jnp.where(slots < 0, -1, slots % slot_width)
    idx = jnp.stack(
        [jnp.where(loop, -1, src_local), jnp.where(loop, -1, dst_index), src_local, dst_index, peer, within, loop.astype(jnp.int32), peer]
    )
    zero = jnp.zeros_like(root_live)
    flt = jnp.stack([root_live, weight_live] + [zero] * 6)
    flat_row = row_lists.reshape(1, -1)
    ground_rows = ground.reshape(num_rows // LANES, LANES)
    list8 = jnp.pad(row_lists, ((0, 0), (0, LANES - slot_width)), constant_values=-1)
    stage = functools.partial(
        run_stage, peers=blocks, slot=slot_width, num_rows=num_rows, columns=columns, num_edges=num_edges
    )
    common = (row_lists, idx, flt, flat_row, ground_rows)
    direction, residual, inverse, flows = stage(0, operands=(sketch_cols,) + common + (list8,))
    state = (residual, direction, inverse)
    for step_idx in range(1, ITERS):
        if step_idx < ITERS - 1:
            direction, residual, solution, flows = stage(step_idx, operands=(flows,) + common + state)
            state = (residual, direction, inverse, solution)
        else:
            solution, gaps = stage(step_idx, operands=(flows,) + common + state)
    resistance = live_mask * gaps.reshape(-1) / columns
    return (solution, resistance)


def solution(mesh):
    in_specs = (
        P(("vtx", "edg"), None),
        P(("vtx", "edg")),
        P("vtx"),
        P(("vtx", "edg")),
        P(("vtx", "edg")),
        P(("vtx", "edg"), None, None),
        P(("vtx", "edg")),
    )
    out_specs = (P("vtx", None), P(("vtx", "edg")))
    return jax.shard_map(local, mesh=mesh, in_specs=in_specs, out_specs=out_specs, check_vma=False)
```

```python
import functools

import jax
import jax.numpy as jnp
from jax import lax
from jax.experimental import pallas as pl
from jax.experimental.pallas import tpu as pltpu
from jax.sharding import PartitionSpec as P

ITERS = 3

lam_low = 0.05
lam_high = 2.0
LANES = 128
VMEM_LIMIT = 60 * 1024 * 1024


def chebyshev_terms(steps):
    centre = (lam_high + lam_low) / 2.0
    half_width = (lam_high - lam_low) / 2.0
    sigma_val = centre / half_width
    rho_prev = 1.0 / sigma_val
    pairs = []
    for count_idx in range(steps - 1):
        rho_next = 1.0 / (2.0 * sigma_val - rho_prev)
        pairs.append((rho_next * rho_prev, 2.0 * rho_next / half_width))
        rho_prev = rho_next
    return (1.0 / centre, pairs)


def split2(x):
    hi = x.astype(jnp.bfloat16)
    lo = (x - hi.astype(jnp.float32)).astype(jnp.bfloat16)
    return hi, lo


def split3(x):
    hi = x.astype(jnp.bfloat16)
    rest = x - hi.astype(jnp.float32)
    mid, lo = split2(rest)
    return hi, mid, lo


def signed(src, dst, shape, axis):
    at = lax.broadcasted_iota(jnp.int16, shape, axis)
    one, none = jnp.ones(shape, jnp.bfloat16), jnp.zeros(shape, jnp.bfloat16)
    is_src = at == jnp.broadcast_to(src.astype(jnp.int16), shape)
    is_dst = at == jnp.broadcast_to(dst.astype(jnp.int16), shape)
    return jnp.where(is_src, one, jnp.where(is_dst, -one, none))


def halves(x):
    n = x.shape[1] // 2
    return x[:, :n] + x[:, n:]


def dot(a, b):
    return jnp.dot(a, b, preferred_element_type=jnp.float32)


def even_piece(total, most):
    return max(n for n in range(8, most + 1, 8) if total % n == 0)


def slot_copy(src, dst, send_sem, recv_sem, target):
    return pltpu.make_async_remote_copy(
        src_ref=src, dst_ref=dst, send_sem=send_sem, recv_sem=recv_sem,
        device_id=target, device_id_type=pl.DeviceIdType.MESH,
    )


def all_to_all(me, peers, src, dst, send_sem, recv_sem):
    for off in range(1, peers):
        to = lax.rem(me + off, peers)
        slot_copy(src(to), dst.at[me], send_sem.at[off], recv_sem.at[off], {"vtx": to}).start()


def all_to_all_wait(me, peers, src, dst, send_sem, recv_sem):
    for off in range(1, peers):
        to = lax.rem(me + off, peers)
        origin = lax.rem(me + peers - off, peers)
        slot_copy(src(to), dst.at[origin], send_sem.at[off], recv_sem.at[off], {"vtx": to}).wait()


class LineSum:
    lag_total, lag_pass = 2, 4

    def __init__(self, z, pieces, own, outer, inner, mine, result, send_sem, outer_sem, inner_sem):
        self.z, self.pieces, self.own, self.outer, self.inner = z, pieces, own, outer, inner
        self.mine, self.result, self.send_sem = mine, result, send_sem
        self.outer_sem, self.inner_sem = outer_sem, inner_sem
        self.near = 1 + z // 3

    def copy(self, kind, k, src, dst, sem, target):
        rows = pl.ds(*self.pieces[k])
        return slot_copy(src.at[rows], dst.at[rows], self.send_sem.at[kind, k], sem.at[k], {"edg": target})

    def end_copy(self, k):
        return self.copy(0, k, self.own, self.outer, self.outer_sem, self.near)

    def at_end(self, work):
        pl.when((self.z + 1) // 2 % 2 == 0)(work)

    def at_middle(self, work):
        for side in (0, 1):
            pl.when(self.z == 1 + side)(functools.partial(work, side))

    def send_group(self, ks):
        def work():
            for k in ks:
                self.end_copy(k).start()

        self.at_end(work)

    def step(self, side, t):
        own, outer, inner, mine, result = self.own, self.outer, self.inner, self.mine, self.result
        count = len(self.pieces)
        far, peer = 3 * side, 2 - side
        if t < count:
            rows = pl.ds(*self.pieces[t])
            self.copy(1, t, own, outer, self.outer_sem, far).wait_recv()
            if t % 2 != side:
                mine[rows, :] = own[rows, :] + outer[rows, :]
                self.copy(0, t, mine, inner, self.inner_sem, peer).start()
        k = t - self.lag_total
        if 0 <= k < count and k % 2 == side:
            rows = pl.ds(*self.pieces[k])
            self.copy(0, k, mine, inner, self.inner_sem, peer).wait_recv()
            total = (own[rows, :] + outer[rows, :]) + inner[rows, :]
            mine[rows, :] = total
            self.copy(0, k, mine, inner, self.inner_sem, peer).start()
            self.copy(1, k, mine, outer, self.outer_sem, far).start()
            result[rows, :] = total
        k = t - self.lag_pass
        if 0 <= k < count and k % 2 != side:
            rows = pl.ds(*self.pieces[k])
            self.copy(0, k, mine, inner, self.inner_sem, peer).wait_recv()
            self.copy(1, k, inner, outer, self.outer_sem, far).start()
            result[rows, :] = inner[rows, :]

    def pass_group(self, ts):
        def work(side):
            for t in ts:
                self.step(side, t)

        self.at_middle(work)

    def finish(self):
        count = len(self.pieces)

        def end():
            for k in range(count):
                self.end_copy(k).wait_recv()
                rows = pl.ds(*self.pieces[k])
                self.result[rows, :] = self.outer[rows, :]
            for k in range(count):
                self.end_copy(k).wait_send()

        def middle(side):
            for k in range(count):
                self.copy(0, k, self.mine, self.inner, self.inner_sem, 2 - side).wait_send()
                source = self.mine if k % 2 == side else self.inner
                self.copy(1, k, source, self.outer, self.outer_sem, 3 * side).wait_send()

        self.at_end(end)
        self.at_middle(middle)


def stage_kernel(stage, peers, groups, pieces, *refs):
    first, pairs = chebyshev_terms(ITERS)
    last = stage == ITERS - 1
    refs = list(refs)

    def take(n):
        got = refs[:n]
        del refs[:n]
        return got

    g_ref, rows_smem, idx_ref, flt_ref, list_ref, ground_ref = take(6)
    if stage == 0:
        (list8_ref,) = take(1)
    else:
        res_in, dir_in, inv_in = take(3)
        sol_in = take(1)[0] if stage > 1 else dir_in
    if stage == 0:
        dir_ref, res_ref, inv_ref, gout_ref = take(4)
        listed_from = dir_ref
    elif not last:
        dir_ref, res_ref, sol_ref, gout_ref = take(4)
        listed_from = dir_ref
    else:
        sol_ref, gap_ref = take(2)
        listed_from = sol_ref
    own, outer, inner, mine, result, yhalo, back, listed, landed = take(9)
    idxc, fltc, field, part, retb, acc = take(6)
    back_send, back_recv, land_send, land_recv, line_send, outer_sem, inner_sem = take(7)
    if stage == 0:
        flows, degh, dback, dback_send, dback_recv = take(5)
    else:
        flows = g_ref

    me, z = lax.axis_index("vtx"), lax.axis_index("edg")
    slot, columns = back.shape[1], back.shape[2]
    halo_len = peers * slot
    num_rows = ground_ref.shape[0] * LANES
    num_edges = idx_ref.shape[1]
    etile = min(512, num_edges)
    ktile = min(1024, num_edges)

    barrier = pltpu.get_barrier_semaphore()

    def greet(target):
        pl.semaphore_signal(barrier, inc=1, device_id=target, device_id_type=pl.DeviceIdType.MESH)

    for off in range(1, peers):
        greet({"vtx": lax.rem(me + off, peers)})

    @pl.when(z > 0)
    def _():
        greet({"edg": z - 1})

    @pl.when(z < 3)
    def _():
        greet({"edg": z + 1})

    idxc[...] = idx_ref[...].T
    fltc[...] = flt_ref[...].T

    if stage == 0:

        def make_terms(k, _):
            rows = pl.ds(pl.multiple_of(k * etile, etile), etile)
            terms = fltc[rows, 0:1] * g_ref[rows, :].astype(jnp.float32)
            flows[rows, :] = jnp.concatenate(split2(terms), axis=1)
            return 0

        lax.fori_loop(0, num_edges // etile, make_terms, 0)
        weights = flt_ref[1:2, :]
        lane = lax.broadcasted_iota(jnp.int32, (num_edges, LANES), 1)

        def count_up(high, row, column):
            up = lax.broadcasted_iota(jnp.int32, (high, num_edges), 0)
            picked = jnp.where(up == row, weights, 0.0)
            low = jnp.where(lane == column, 1.0, 0.0).astype(jnp.bfloat16)
            parts = dot(jnp.concatenate(split3(picked), axis=0), low)
            return parts[:high] + parts[high : 2 * high] + parts[2 * high :]

        high = num_rows // LANES
        up_rows = -(-high // 16) * 16
        degree_own = count_up(up_rows, idx_ref[2:3, :] // LANES, idxc[:, 2:3] % LANES)
        degree_own += count_up(up_rows, idx_ref[3:4, :] // LANES, idxc[:, 3:4] % LANES)
        own[num_rows:, :] = degree_own[:high]
        degree_far = count_up(-(-peers // 16) * 16, idx_ref[4:5, :], idxc[:, 5:6])
        for q in range(peers):
            degh[q] = jnp.broadcast_to(degree_far[q : q + 1, :], (8, LANES))

    def scatter_rows(at, rows):
        acc[:rows, :] = jnp.zeros((rows, 2 * columns), jnp.float32)

        def body(k, _):
            cols = pl.ds(pl.multiple_of(k * ktile, ktile), ktile)
            pick = signed(idx_ref[0:1, cols] - at, idx_ref[1:2, cols] - at, (rows, ktile), 0)
            acc[:rows, :] += dot(pick, flows[cols, :])
            return 0

        lax.fori_loop(0, num_edges // ktile, body, 0)
        return halves(acc[:rows, :])

    hpiece = even_piece(halo_len, 512)
    for at in range(0, halo_len, hpiece):
        yhalo[at : at + hpiece, :] = scatter_rows(num_rows + at, hpiece)

    pl.semaphore_wait(barrier, peers + (z + 1) // 2 % 2)

    def halo_of(to):
        return yhalo.at[pl.ds(pl.multiple_of(to * slot, 8), slot)]

    def degree_of(to):
        return degh.at[to]

    all_to_all(me, peers, halo_of, back, back_send, back_recv)
    back[me] = yhalo[pl.ds(pl.multiple_of(me * slot, 8), slot), :]
    if stage == 0:
        all_to_all(me, peers, degree_of, dback, dback_send, dback_recv)
        dback[me] = degh[me]

    line = LineSum(z, pieces, own, outer, inner, mine, result, line_send, outer_sem, inner_sem)
    for c, (at, size, ks) in enumerate(groups):
        local_sum = scatter_rows(at, size)
        if c == 0:
            all_to_all_wait(me, peers, halo_of, back, back_send, back_recv)
            retb[...] = jnp.concatenate(split2(back[...].reshape(halo_len, columns)), axis=1)
            if stage == 0:
                all_to_all_wait(me, peers, degree_of, dback, dback_send, dback_recv)
                cols8 = list8_ref[...].T
                up = lax.broadcasted_iota(jnp.int32, (high, LANES), 0)
                lane = lax.broadcasted_iota(jnp.int32, (LANES, LANES), 1)
                for q in range(peers):
                    picked = jnp.where(up == list8_ref[q : q + 1, :] // LANES, dback[q, 0:1, :], 0.0)
                    low = jnp.where(lane == cols8[:, q : q + 1] % LANES, 1.0, 0.0).astype(jnp.bfloat16)
                    parts = dot(jnp.concatenate(split3(picked), axis=0), low)
                    own[num_rows:, :] += parts[:high] + parts[high : 2 * high] + parts[2 * high :]
        row = lax.broadcasted_iota(jnp.int32, (size, halo_len), 0)
        pick = jnp.where(row == list_ref[...] - at, 1.0, 0.0).astype(jnp.bfloat16)
        own[at : at + size, :] = local_sum + halves(dot(pick, retb[...]))
        line.send_group(ks)
        if c > 0:
            line.pass_group(groups[c - 1][2])
    line.pass_group(list(groups[-1][2]) + list(range(len(pieces), len(pieces) + line.lag_pass)))
    line.finish()

    ground_cols = ground_ref[...].T
    if stage == 0:
        inverse = 1.0 / (result[num_rows:, :] + ground_ref[...])
        inv_ref[...] = inverse
    else:
        inverse = inv_in[...]
    inverse_cols = inverse.T
    for at in range(0, num_rows, LANES):
        rows = slice(at, at + LANES)
        j = at // LANES
        inv_col, ground_col = inverse_cols[:, j : j + 1], ground_cols[:, j : j + 1]
        if stage == 0:
            res_ref[rows, :] = result[rows, :]
            shown = first * inv_col * result[rows, :]
            dir_ref[rows, :] = shown
        else:
            keep_coef, push_coef = pairs[stage - 1]
            residual = res_in[rows, :] - (ground_col * dir_in[rows, :] + result[rows, :])
            direction = keep_coef * dir_in[rows, :] + push_coef * inv_col * residual
            total = sol_in[rows, :] + direction
            sol_ref[rows, :] = total
            shown = total
            if not last:
                res_ref[rows, :] = residual
                dir_ref[rows, :] = direction
                shown = direction
        field[rows, :] = jnp.concatenate(split2(shown), axis=1)

    def pick_rows(h, _):
        for q in range(peers):
            listed[q, pl.ds(h, 1), :] = listed_from[pl.ds(rows_smem[q, h], 1), :]
        return 0

    lax.fori_loop(0, slot, pick_rows, 0)

    def listed_of(to):
        return listed.at[to]

    all_to_all(me, peers, listed_of, landed, land_send, land_recv)
    landed[me] = listed[me]

    def gather_near(k, _):
        rows = pl.ds(pl.multiple_of(k * etile, etile), etile)
        d = signed(idxc[rows, 0:1], idxc[rows, 1:2], (etile, num_rows), 1)
        part[rows, :] = halves(dot(d, field[:num_rows, :]))
        return 0

    lax.fori_loop(0, num_edges // etile, gather_near, 0)
    all_to_all_wait(me, peers, listed_of, landed, land_send, land_recv)
    field[num_rows:, :] = jnp.concatenate(split2(landed[...].reshape(halo_len, columns)), axis=1)

    def gather_far(k):
        rows = pl.ds(k * etile, etile)
        d = signed(idxc[rows, 0:1] - num_rows, idxc[rows, 1:2] - num_rows, (etile, halo_len), 1)
        return rows, part[rows, :] + halves(dot(d, field[num_rows:, :]))

    if not last:

        def make_flows(k, _):
            k = pl.multiple_of(k * etile, etile) // etile
            rows, gap = gather_far(k)
            gout_ref[rows, :] = jnp.concatenate(split2(gap * fltc[rows, 1:2]), axis=1)
            return 0

        lax.fori_loop(0, num_edges // etile, make_flows, 0)
    else:
        lane = lax.broadcasted_iota(jnp.int32, (LANES, LANES), 1)
        wide = num_edges // LANES
        for base in range(0, wide, LANES):
            sums = jnp.zeros((LANES, LANES), jnp.float32)
            for k in range(base * LANES // etile, min(wide, base + LANES) * LANES // etile):
                _, gap = gather_far(k)
                square = jnp.sum(gap * gap, axis=1, keepdims=True)
                for i in range(etile // LANES):
                    j = k * (etile // LANES) + i - base
                    sums = jnp.where(lane == j, square[i * LANES : (i + 1) * LANES, :], sums)
            take_rows = min(LANES, wide - base)
            gap_ref[base : base + take_rows, :] = sums.T[:take_rows, :]


def run_stage(stage, peers, slot, num_rows, columns, num_edges, operands):
    high = num_rows // LANES
    extra = high if stage == 0 else 0
    size, big = 128, 512
    pieces = [(at, size) for at in range(0, num_rows, size)]
    groups = [[at, big, list(range(at // size, (at + big) // size))] for at in range(0, num_rows, big)]
    if extra:
        groups[-1][2].append(len(pieces))
        pieces.append((num_rows, extra))
    count = len(pieces)
    f32, bf16, i32 = jnp.float32, jnp.bfloat16, jnp.int32
    halo_len = peers * slot
    field = jax.ShapeDtypeStruct((num_rows, columns), f32)
    flows = jax.ShapeDtypeStruct((num_edges, 2 * columns), bf16)
    if stage == 0:
        outs = [field, field, jax.ShapeDtypeStruct((high, LANES), f32), flows]
    elif stage < ITERS - 1:
        outs = [field, field, field, flows]
    else:
        outs = [field, jax.ShapeDtypeStruct((num_edges // LANES, LANES), f32)]
    vmem = pl.BlockSpec(memory_space=pltpu.VMEM)
    in_specs = [vmem] * len(operands)
    in_specs[1] = pl.BlockSpec(memory_space=pltpu.SMEM)
    dma = pltpu.SemaphoreType.DMA
    buffer = pltpu.VMEM((num_rows + extra, columns), f32)
    halo = pltpu.VMEM((peers, slot, columns), f32)
    scratch = [buffer] * 5 + [pltpu.VMEM((halo_len, columns), f32)] + [halo] * 3
    scratch += [pltpu.VMEM((num_edges, 8), i32), pltpu.VMEM((num_edges, 8), f32)]
    scratch += [pltpu.VMEM((num_rows + halo_len, 2 * columns), bf16), pltpu.VMEM((num_edges, columns), f32)]
    scratch += [pltpu.VMEM((halo_len, 2 * columns), bf16), pltpu.VMEM((big, 2 * columns), f32)]
    scratch += [dma((peers,))] * 4 + [dma((2, count)), dma((count,)), dma((count,))]
    if stage == 0:
        scratch += [pltpu.VMEM((num_edges, 2 * columns), bf16)]
        scratch += [pltpu.VMEM((peers, 8, LANES), f32)] * 2 + [dma((peers,)), dma((peers,))]
    return pl.pallas_call(
        functools.partial(stage_kernel, stage, peers, groups, pieces),
        in_specs=in_specs,
        out_specs=[vmem] * len(outs),
        out_shape=outs,
        scratch_shapes=scratch,
        compiler_params=pltpu.CompilerParams(collective_id=stage, has_side_effects=True, vmem_limit_bytes=VMEM_LIMIT),
        name="stage%d" % stage,
    )(*operands)


def local(sketch_cols, edge_weight, ground, src_local, dst_index, send_rows, edge_count):
    blocks = lax.axis_size("vtx")
    num_rows = ground.shape[0]
    num_edges = edge_weight.shape[0]
    slot_width = send_rows.shape[2]
    columns = sketch_cols.shape[1]
    row_lists = send_rows[0]
    live_mask = (jnp.arange(num_edges, dtype=jnp.int32) < edge_count[0]).astype(jnp.float32)
    weight_live = edge_weight * live_mask
    root_live = jnp.sqrt(edge_weight) * live_mask
    loop = src_local == dst_index
    slots = dst_index - num_rows
    peer = jnp.where(slots < 0, -1, slots // slot_width)
    within = jnp.where(slots < 0, -1, slots % slot_width)
    idx = jnp.stack(
        [jnp.where(loop, -1, src_local), jnp.where(loop, -1, dst_index), src_local, dst_index, peer, within, loop.astype(jnp.int32), peer]
    )
    zero = jnp.zeros_like(root_live)
    flt = jnp.stack([root_live, weight_live] + [zero] * 6)
    flat_row = row_lists.reshape(1, -1)
    ground_rows = ground.reshape(num_rows // LANES, LANES)
    list8 = jnp.pad(row_lists, ((0, 0), (0, LANES - slot_width)), constant_values=-1)
    stage = functools.partial(
        run_stage, peers=blocks, slot=slot_width, num_rows=num_rows, columns=columns, num_edges=num_edges
    )
    common = (row_lists, idx, flt, flat_row, ground_rows)
    direction, residual, inverse, flows = stage(0, operands=(sketch_cols,) + common + (list8,))
    state = (residual, direction, inverse)
    for step_idx in range(1, ITERS):
        if step_idx < ITERS - 1:
            direction, residual, solution, flows = stage(step_idx, operands=(flows,) + common + state)
            state = (residual, direction, inverse, solution)
        else:
            solution, gaps = stage(step_idx, operands=(flows,) + common + state)
    resistance = live_mask * gaps.reshape(-1) / columns
    return (solution, resistance)


def solution(mesh):
    in_specs = (
        P(("vtx", "edg"), None),
        P(("vtx", "edg")),
        P("vtx"),
        P(("vtx", "edg")),
        P(("vtx", "edg")),
        P(("vtx", "edg"), None, None),
        P(("vtx", "edg")),
    )
    out_specs = (P("vtx", None), P(("vtx", "edg")))
    return jax.shard_map(local, mesh=mesh, in_specs=in_specs, out_specs=out_specs, check_vma=False)
```
